32 devices in a mesh: occ: 8 (over z, y), vir: 4 (over x, core).
Axes of the slice: x: 2, y: 2, z: 4, core: 2. Of those that a mesh axis runs over, the one named last changes fastest.
Arguments:
- amplitudes: bfloat16 [16384, 8192], P('occ', 'vir'), may hold values from -6 to 6
- integrals: bfloat16 [8192, 8192], P('occ', 'vir'), may hold values from -0.0625 to 0.0625
- other_terms: bfloat16 [16384, 8192], P('occ', 'vir'), may hold values from -6 to 6
- occ_irrep: int32 [4], replicated, may hold values from 0 to 3, as said below
- vir_irrep: int32 [32], replicated, may hold values from 0 to 3
- pair_tiles: int32 [8, 2], replicated, may hold values from 0 to 31
- spin_mask: int32 [16, 8], replicated, may hold values 0 or 1
- occ_energy: float32 [128], replicated, may hold values from -2 to -0.5
- vir_energy: float32 [1024], replicated, may hold values from 0.2 to 3
Outputs:
- updated: bfloat16 [16384, 8192], P('occ', 'vir')
The draws below stay inside these ranges and needn't reach their ends.
Inputs may be any that keep to these rules, and one draw needn't show every extreme that they name: `occ_irrep`: the labels are not all equal. `pair_tiles`: tiles of one pair may repeat across pairs.
All inputs are finite; a program needn't handle non-finite values.
Results may differ from the reference program's by a relative error of at most 0.001.
Values may be sent and summed in bfloat16 or wider, within the bound.
A program may use at most 448 MiB of HBM per device.

```python
import jax
import jax.numpy as jnp
from jax import lax

OCC = 128
VIR = 1024
TILE = 32
NPAIR = 8
IRREPS = 4
OTILES = 4
VTILES = 32
OPAIRS = 16384
VPAIRS = 8192


def draw_occ_irrep(key, part):
    first_key = jax.random.fold_in(key, 11)
    second_key = jax.random.fold_in(key, 23)
    labels = jax.random.randint(first_key, (OTILES,), 0, IRREPS).astype(jnp.int32)
    offset = jax.random.randint(second_key, (), 1, IRREPS).astype(jnp.int32)
    return labels.at[1].set(jnp.bitwise_xor(labels[0], offset))


def touch_ends(values, own_key, smallest, high):
    longest = values.shape.index(max(values.shape))
    spots = []
    for shift in (0, 1):
        where = [jax.random.randint(jax.random.fold_in(own_key, axis), (), 0, length) for axis, length in enumerate(values.shape)]
        where[longest] = (where[longest] + shift) % values.shape[longest]
        spots.append(tuple(where))
    return values.at[spots[0]].set(smallest).at[spots[1]].set(high)


def block_levels(rng, extent, split, low, high):
    factor_of = 1.0
    for position, blocks in split:
        draws = jax.random.uniform(jax.random.fold_in(jax.random.fold_in(rng, 6), position), (blocks,), jnp.float32, low / len(split), high / len(split))
        factor_of = factor_of * jnp.repeat(jnp.exp(draws), extent[position] // blocks).reshape((-1,) + (1,) * (len(extent) - 1 - position))
    return factor_of


def gaussian(own_key, extent, width, bound, split=(), kind=jnp.bfloat16):
    level = block_levels(own_key, extent, split, -0.22, 0.18) if split else 1.0
    entries = jax.random.normal(own_key, extent, jnp.float32) * width * level
    return jnp.minimum(jnp.maximum(entries, -bound), bound).astype(kind)


def setup_inputs(seed: int = 0) -> dict:
    seeds = jax.random.split(jax.random.key(seed), 10)
    return {
        "amplitudes": gaussian(seeds[0], (OPAIRS, VPAIRS), 1.0, 6.0, ((0, 8), (1, 4))),
        "integrals": gaussian(seeds[1], (VPAIRS, VPAIRS), VPAIRS ** -0.5, 0.0625, ((0, 8), (1, 4))),
        "other_terms": gaussian(seeds[2], (OPAIRS, VPAIRS), 1.0, 6.0, ((0, 8), (1, 4))),
        "occ_irrep": draw_occ_irrep(jax.random.fold_in(seeds[9], 71), 0),
        "vir_irrep": touch_ends(jax.random.randint(seeds[4], (VTILES,), 0, IRREPS), jax.random.fold_in(seeds[4], 1), 0, IRREPS - 1).astype(jnp.int32),
        "pair_tiles": touch_ends(jax.random.randint(seeds[5], (NPAIR, 2), 0, VTILES), jax.random.fold_in(seeds[5], 1), 0, VTILES - 1).astype(jnp.int32),
        "spin_mask": touch_ends((jax.random.randint(seeds[6], (OTILES * OTILES, NPAIR), 0, 4) < 3).astype(jnp.int32), jax.random.fold_in(seeds[6], 1), 0, 1),
        "occ_energy": jnp.clip(jax.random.uniform(seeds[7], (OCC,), jnp.float32, -2.0, -0.5), -2.0, -0.5),
        "vir_energy": jnp.clip(jax.random.uniform(seeds[8], (VIR,), jnp.float32, 0.2, 3.0), 0.2, 3.0),
    }


def lookup(index, table):
    hits = index[:, None] == jnp.arange(table.shape[0], dtype=jnp.int32)[None, :]
    return jnp.sum(jnp.where(hits[:, :, None], table[None, :, :], jnp.zeros_like(table)[None, :, :]), axis=1)


def symmetry(occ_irrep, vir_irrep, pair_tiles, spin_mask):
    first = lookup(pair_tiles[:, 0], vir_irrep[:, None])[:, 0]
    second = lookup(pair_tiles[:, 1], vir_irrep[:, None])[:, 0]
    pair_irrep = jnp.bitwise_xor(first, second)
    occ_pair = jnp.bitwise_xor(occ_irrep[:, None], occ_irrep[None, :]).reshape(-1)
    allowed = jnp.where((occ_pair[:, None] == pair_irrep[None, :]) & (spin_mask == 1), 1.0, 0.0).astype(jnp.float32)
    coupled = jnp.where(pair_irrep[:, None] == pair_irrep[None, :], 1.0, 0.0).astype(jnp.float32)
    return allowed, coupled


def reference(amplitudes, integrals, other_terms, occ_irrep, vir_irrep, pair_tiles, spin_mask, occ_energy, vir_energy):
    allowed, coupled = symmetry(occ_irrep, vir_irrep, pair_tiles, spin_mask)
    square = TILE * TILE
    occ_blocks = OTILES * OTILES
    amp_four = amplitudes.reshape(occ_blocks, square, NPAIR, square)
    masked_amp = jnp.where(allowed[:, None, :, None] > 0.5, amp_four, jnp.zeros_like(amp_four)).reshape(OPAIRS, VPAIRS)
    int_four = integrals.reshape(NPAIR, square, NPAIR, square)
    masked_int = jnp.where(coupled[:, None, :, None] > 0.5, int_four, jnp.zeros_like(int_four)).reshape(VPAIRS, VPAIRS)
    height = min(512, OPAIRS)
    stacked = masked_amp.reshape(OPAIRS // height, height, VPAIRS)
    ladder = lax.map(lambda rows_block: jnp.dot(rows_block, masked_int, preferred_element_type=jnp.float32), stacked)
    ladder = ladder.reshape(occ_blocks, square, NPAIR, square)
    occ_tiles = occ_energy.reshape(OTILES, TILE)
    pair_occ = (occ_tiles[:, None, :, None] + occ_tiles[None, :, None, :]).reshape(occ_blocks, square)
    vir_tiles = vir_energy.reshape(VTILES, TILE)
    first = lookup(pair_tiles[:, 0], vir_tiles)
    second = lookup(pair_tiles[:, 1], vir_tiles)
    pair_vir = (first[:, :, None] + second[:, None, :]).reshape(NPAIR, square)
    denom = pair_occ[:, :, None, None] - pair_vir[None, None, :, :]
    other = other_terms.astype(jnp.float32).reshape(occ_blocks, square, NPAIR, square)
    updated = allowed[:, None, :, None] * ((ladder + other) / denom)
    return updated.astype(jnp.bfloat16).reshape(OPAIRS, VPAIRS)
```

```python
import functools

import jax
import jax.numpy as jnp
from jax import lax
from jax.experimental import pallas as pl
from jax.experimental.pallas import tpu as pltpu
from jax.sharding import PartitionSpec as P

TILE = 32
OTILES = 4
SQUARE = TILE * TILE
PIECES = 4
STEP_COLS = 256


def lookup(index, table):
    hits = index[:, None] == jnp.arange(table.shape[0], dtype=jnp.int32)[None, :]
    return jnp.sum(
        jnp.where(hits[:, :, None], table[None, :, :], jnp.zeros_like(table)[None, :, :]), axis=1
    )


def symmetry(occ_irrep, vir_irrep, pair_tiles, spin_mask):
    first = lookup(pair_tiles[:, 0], vir_irrep[:, None])[:, 0]
    second = lookup(pair_tiles[:, 1], vir_irrep[:, None])[:, 0]
    pair_irrep = jnp.bitwise_xor(first, second)
    occ_pair = jnp.bitwise_xor(occ_irrep[:, None], occ_irrep[None, :]).reshape(-1)
    allowed = jnp.where(
        (occ_pair[:, None] == pair_irrep[None, :]) & (spin_mask == 1), 1.0, 0.0
    ).astype(jnp.float32)
    coupled = jnp.where(pair_irrep[:, None] == pair_irrep[None, :], 1.0, 0.0).astype(jnp.float32)
    return (allowed, coupled)


def dense_device(
    amplitudes,
    integrals,
    other_terms,
    occ_irrep,
    vir_irrep,
    pair_tiles,
    spin_mask,
    occ_energy,
    vir_energy,
):
    allowed, coupled = symmetry(occ_irrep, vir_irrep, pair_tiles, spin_mask)
    height = amplitudes.shape[0]
    width = amplitudes.shape[1]
    slab_height = integrals.shape[0]
    row_global = lax.axis_index("occ") * height + jnp.arange(height, dtype=jnp.int32)
    col_global = lax.axis_index("vir") * width + jnp.arange(width, dtype=jnp.int32)
    row_block = row_global // SQUARE
    col_pair = col_global // SQUARE
    row_allowed = lookup(row_block, allowed)
    amp_keep = lookup(col_pair, row_allowed.T).T
    masked_amp = jnp.where(amp_keep > 0.5, amplitudes, jnp.zeros_like(amplitudes))
    slab_pair = (
        lax.axis_index("occ") * slab_height + jnp.arange(slab_height, dtype=jnp.int32)
    ) // SQUARE
    int_keep = lookup(col_pair, lookup(slab_pair, coupled).T).T
    masked_slab = jnp.where(int_keep > 0.5, integrals, jnp.zeros_like(integrals))
    whole_amp = lax.all_gather(masked_amp, "vir", axis=1, tiled=True)
    whole_slab = lax.all_gather(masked_slab, "occ", axis=0, tiled=True)
    ladder = jnp.dot(whole_amp, whole_slab, preferred_element_type=jnp.float32)
    inner = row_global % SQUARE
    occ_first = row_block // OTILES * TILE + inner // TILE
    occ_second = row_block % OTILES * TILE + inner % TILE
    occ_sum = (
        lookup(occ_first, occ_energy[:, None])[:, 0] + lookup(occ_second, occ_energy[:, None])[:, 0]
    )
    col_inner = col_global % SQUARE
    tile_first = lookup(col_pair, pair_tiles[:, 0:1])[:, 0]
    tile_second = lookup(col_pair, pair_tiles[:, 1:2])[:, 0]
    vir_first = tile_first * TILE + col_inner // TILE
    vir_second = tile_second * TILE + col_inner % TILE
    vir_sum = (
        lookup(vir_first, vir_energy[:, None])[:, 0] + lookup(vir_second, vir_energy[:, None])[:, 0]
    )
    denom = occ_sum[:, None] - vir_sum[None, :]
    updated = amp_keep * ((ladder + other_terms.astype(jnp.float32)) / denom)
    return updated.astype(jnp.bfloat16)


def pack_kernel(index_ref, block_ref, slot_ref):
    slot_ref[0] = block_ref[...]


def pack(index, array, slots):
    half = SQUARE // 2
    return pl.pallas_call(
        pack_kernel,
        out_shape=jax.ShapeDtypeStruct((slots, SQUARE, SQUARE), array.dtype),
        grid_spec=pltpu.PrefetchScalarGridSpec(
            num_scalar_prefetch=1,
            grid=(slots, 2),
            in_specs=[
                pl.BlockSpec((half, SQUARE), lambda j, r, ix: (ix[j] // 2 * 2 + r, ix[j] % 2))
            ],
            out_specs=pl.BlockSpec((1, half, SQUARE), lambda j, r, ix: (j, r, 0)),
        ),
        name="pack",
    )(index, array)


def exchange_kernel(
    n, cap_a, cap_b, a_ref, b_ref, ag_ref, bg_ref, own_sem, a_send, a_recv, b_send, b_recv
):
    o = lax.axis_index("occ")
    v = lax.axis_index("vir")

    def place(pos):
        late = pos // (n // 2)
        return 2 * pos * (1 - late) + (2 * (n - 1 - pos) + 1) * late

    odd = o % 2
    pos = (o // 2) * (1 - odd) + (n - 1 - o // 2) * odd
    right = place((pos + 1) % n)
    left = place((pos + n - 1) % n)
    mate = v + 1 - 2 * (v % 2)
    across = (v + 2) % 4
    mesh_id = pl.DeviceIdType.MESH

    barrier = pltpu.get_barrier_semaphore()
    for target in ((right, v), (left, v), (o, mate), (o, across)):
        pl.semaphore_signal(barrier, inc=1, device_id=target, device_id_type=mesh_id)
    pl.semaphore_wait(barrier, 4)

    def a_copy(which, src, owner, target):
        return pltpu.make_async_remote_copy(
            src_ref=src,
            dst_ref=ag_ref.at[owner, pl.ds(0, cap_a)],
            send_sem=a_send.at[which],
            recv_sem=a_recv.at[which],
            device_id=(o, target),
            device_id_type=mesh_id,
        )

    rows = SQUARE // PIECES

    def b_copy(step, piece):
        cut = pl.ds(piece * rows, rows)
        if piece < PIECES // 2:
            owner, target = place((pos + n - step) % n), right
        else:
            owner, target = place((pos + step) % n), left
        src = b_ref.at[:, cut] if step == 0 else bg_ref.at[owner, pl.ds(0, cap_b), cut]
        return pltpu.make_async_remote_copy(
            src_ref=src,
            dst_ref=bg_ref.at[owner, pl.ds(0, cap_b), cut],
            send_sem=b_send.at[step, piece],
            recv_sem=b_recv.at[step, piece],
            device_id=(target, v),
            device_id_type=mesh_id,
        )

    order = [p for pair in zip(range(PIECES // 2), range(PIECES // 2, PIECES)) for p in pair]
    b_copies = {}
    for piece in order:
        b_copies[0, piece] = b_copy(0, piece)
        b_copies[0, piece].start()
    to_across = a_copy(0, a_ref, v, across)
    to_across.start()
    to_mate = a_copy(1, a_ref, v, mate)
    to_mate.start()
    own_b = pltpu.make_async_copy(b_ref, bg_ref.at[o, pl.ds(0, cap_b)], own_sem.at[0])
    own_b.start()
    own_a = pltpu.make_async_copy(a_ref, ag_ref.at[v, pl.ds(0, cap_a)], own_sem.at[1])
    own_a.start()
    for step in range(1, n - 1):
        for piece in order:
            b_copies[step - 1, piece].wait_recv()
            b_copies[step, piece] = b_copy(step, piece)
            b_copies[step, piece].start()
    to_across.wait_recv()
    forward = a_copy(2, ag_ref.at[across, pl.ds(0, cap_a)], across, mate)
    forward.start()
    for piece in order:
        b_copies[n - 2, piece].wait_recv()
    to_mate.wait_recv()
    forward.wait_recv()
    for step in range(n - 1):
        for piece in order:
            b_copies[step, piece].wait_send()
    to_across.wait_send()
    to_mate.wait_send()
    forward.wait_send()
    own_b.wait()
    own_a.wait()


def exchange(n, which, cap_a, cap_b, amplitudes, integrals, a_index, b_index):
    packed_a = pack(a_index, amplitudes, cap_a)
    packed_b = pack(b_index, integrals, cap_b)
    any_spec = pl.BlockSpec(memory_space=pl.ANY)
    return pl.pallas_call(
        functools.partial(exchange_kernel, n, cap_a, cap_b),
        out_shape=(
            jax.ShapeDtypeStruct((4, 4, SQUARE, SQUARE), amplitudes.dtype),
            jax.ShapeDtypeStruct((n, 2, SQUARE, SQUARE), integrals.dtype),
        ),
        in_specs=[any_spec, any_spec],
        out_specs=(any_spec, any_spec),
        scratch_shapes=[
            pltpu.SemaphoreType.DMA((2,)),
            pltpu.SemaphoreType.DMA((3,)),
            pltpu.SemaphoreType.DMA((3,)),
            pltpu.SemaphoreType.DMA((n - 1, PIECES)),
            pltpu.SemaphoreType.DMA((n - 1, PIECES)),
        ],
        compiler_params=pltpu.CompilerParams(collective_id=which, has_side_effects=True),
        name="exchange",
    )(packed_a, packed_b)


def ladder_kernel(
    count_ref, keep_ref, a_slot, b_slot, a_ref, b_ref, other_ref, occ_ref, vir_ref, out_ref, acc
):
    block = pl.program_id(0)
    step = pl.program_id(1)
    count = count_ref[block]
    a_block = a_ref.at[0]
    b_block = b_ref.at[0]

    @pl.when(step == 0)
    def _():
        acc[...] = jnp.zeros_like(acc)

    @pl.when(step < count)
    def _():
        @pl.loop(0, SQUARE // STEP_COLS)
        def _(part):
            cols = pl.ds(pl.multiple_of(part * STEP_COLS, STEP_COLS), STEP_COLS)
            acc[:, cols] += jnp.dot(
                a_block[...], b_block[:, cols], preferred_element_type=jnp.float32
            )

    last = step == pl.num_programs(1) - 1

    @pl.when(last & (keep_ref[block] == 1))
    def _():
        @pl.loop(0, SQUARE // 128)
        def _(part):
            cut = pl.ds(pl.multiple_of(part * 128, 128), 128)
            denom = occ_ref[0, cut, :] - vir_ref[0]
            total = acc[cut, :] + other_ref[cut, :].astype(jnp.float32)
            out_ref[cut, :] = (total / denom).astype(out_ref.dtype)

    @pl.when(last & (keep_ref[block] == 0))
    def _():
        out_ref[...] = jnp.zeros_like(out_ref)


def ladder(count, keep, a_slot, b_slot, steps, a_all, b_all, other_terms, occ_sum, vir_sum):
    square = (SQUARE, SQUARE)
    return pl.pallas_call(
        ladder_kernel,
        out_shape=jax.ShapeDtypeStruct(other_terms.shape, other_terms.dtype),
        grid_spec=pltpu.PrefetchScalarGridSpec(
            num_scalar_prefetch=4,
            grid=(4, steps),
            in_specs=[
                pl.BlockSpec((1,) + square, lambda b, j, c, k, sa, sb: (sa[b * steps + j], 0, 0)),
                pl.BlockSpec((1,) + square, lambda b, j, c, k, sa, sb: (sb[b * steps + j], 0, 0)),
                pl.BlockSpec(square, lambda b, j, c, k, sa, sb: (b // 2, b % 2)),
                pl.BlockSpec((1, SQUARE, 1), lambda b, j, c, k, sa, sb: (b // 2, 0, 0)),
                pl.BlockSpec((1, 1, SQUARE), lambda b, j, c, k, sa, sb: (b % 2, 0, 0)),
            ],
            out_specs=pl.BlockSpec(square, lambda b, j, c, k, sa, sb: (b // 2, b % 2)),
            scratch_shapes=[pltpu.VMEM(square, jnp.float32)],
        ),
        compiler_params=pltpu.CompilerParams(vmem_limit_bytes=48 << 20),
        name="ladder",
    )(count, keep, a_slot, b_slot, a_all, b_all, other_terms, occ_sum, vir_sum)


def ranks(flags):
    size = flags.shape[-1]
    before = jnp.arange(size)[:, None] < jnp.arange(size)[None, :]
    return jnp.sum(jnp.where(before, flags[..., :, None], 0), axis=-2)


def pick(flags, rank, values, size):
    total = jnp.sum(flags, axis=-1, keepdims=True)
    want = jnp.minimum(jnp.arange(size), jnp.maximum(total - 1, 0))
    hit = (flags[..., :, None] == 1) & (rank[..., :, None] == want[..., None, :])
    return jnp.sum(jnp.where(hit, values[..., :, None], 0), axis=-2)


def block_device(
    amplitudes,
    integrals,
    other_terms,
    occ_irrep,
    vir_irrep,
    pair_tiles,
    spin_mask,
    occ_energy,
    vir_energy,
):
    o = lax.axis_index("occ")
    v = lax.axis_index("vir")
    allowed, _ = symmetry(occ_irrep, vir_irrep, pair_tiles, spin_mask)
    allowed = allowed.astype(jnp.int32)
    pairs = allowed.shape[1]
    occ_devices = allowed.shape[0] // 2
    used = jnp.max(allowed[:, :, None] * allowed[:, None, :], axis=0)
    a_flags = allowed.reshape(occ_devices, 2, 4, 2).transpose(0, 2, 1, 3).reshape(occ_devices, 4, 4)
    b_flags = used.reshape(pairs, 4, 2)
    a_most = jnp.max(jnp.sum(a_flags, axis=-1))
    b_most = jnp.max(jnp.sum(b_flags, axis=-1))

    a_here = lax.dynamic_index_in_dim(a_flags, o, 0, keepdims=False)
    a_rank = ranks(a_here)
    b_here = lax.dynamic_index_in_dim(b_flags, v, 1, keepdims=False)
    b_rank = ranks(b_here)
    a_mine = lax.dynamic_index_in_dim(a_here, v, 0, keepdims=False)
    b_mine = lax.dynamic_index_in_dim(b_here, o, 0, keepdims=False)
    a_index = pick(a_mine, ranks(a_mine), jnp.arange(4, dtype=jnp.int32), 4)
    b_index = pick(b_mine, ranks(b_mine), jnp.arange(2, dtype=jnp.int32), 2)

    variant = jnp.where(b_most > 1, 2, jnp.where(a_most > 2, 1, 0))
    run = functools.partial(exchange, occ_devices)
    a_all, b_all = lax.switch(
        variant,
        [
            functools.partial(run, 0, 2, 1),
            functools.partial(run, 1, 4, 1),
            functools.partial(run, 2, 4, 2),
        ],
        amplitudes,
        integrals,
        a_index,
        b_index,
    )

    a_rows = a_here.reshape(4, 2, 2).transpose(1, 0, 2).reshape(2, pairs)
    a_at = (a_rank + 4 * jnp.arange(4, dtype=jnp.int32)[:, None]).reshape(4, 2, 2)
    a_at = a_at.transpose(1, 0, 2).reshape(2, pairs)
    b_at = (b_rank + 2 * jnp.arange(pairs, dtype=jnp.int32)[:, None]).T
    keep = a_mine.reshape(2, 2)
    terms = a_rows[:, None, :] * keep[:, :, None]
    order = ranks(terms)
    a_slot = pick(terms, order, jnp.broadcast_to(a_at[:, None, :], terms.shape), pairs)
    b_slot = pick(terms, order, jnp.broadcast_to(b_at[None, :, :], terms.shape), pairs)
    count = jnp.sum(terms, axis=-1).reshape(-1)

    occ_tiles = occ_energy.reshape(OTILES, TILE)
    pair_occ = (occ_tiles[:, None, :, None] + occ_tiles[None, :, None, :]).reshape(-1, SQUARE)
    occ_sum = lax.dynamic_slice_in_dim(pair_occ, 2 * o, 2, 0)[:, :, None]
    vir_tiles = vir_energy.reshape(-1, TILE)
    tiles = lax.dynamic_slice_in_dim(pair_tiles, 2 * v, 2, 0)
    first = lookup(tiles[:, 0], vir_tiles)
    second = lookup(tiles[:, 1], vir_tiles)
    vir_sum = (first[:, :, None] + second[:, None, :]).reshape(2, 1, SQUARE)

    return ladder(
        count,
        keep.reshape(-1),
        a_slot.reshape(-1),
        b_slot.reshape(-1),
        pairs,
        a_all.reshape(-1, SQUARE, SQUARE),
        b_all.reshape(-1, SQUARE, SQUARE),
        other_terms,
        occ_sum,
        vir_sum,
    )


def per_device(amplitudes, integrals, *rest):
    blocks = amplitudes.shape == (2 * SQUARE, 2 * SQUARE)
    blocks = blocks and integrals.shape == (SQUARE, 2 * SQUARE) and lax.axis_size("vir") == 4
    blocks = blocks and lax.axis_size("occ") == OTILES * OTILES // 2
    device = block_device if blocks else dense_device
    return device(amplitudes, integrals, *rest)


def solution(mesh):
    in_specs = (P("occ", "vir"), P("occ", "vir"), P("occ", "vir"), P(), P(), P(), P(), P(), P())
    out_specs = P("occ", "vir")
    return jax.shard_map(
        per_device, mesh=mesh, in_specs=in_specs, out_specs=out_specs, check_vma=False
    )
```

```python
import functools

import jax
import jax.numpy as jnp
from jax import lax
from jax.experimental import pallas as pl
from jax.experimental.pallas import tpu as pltpu
from jax.sharding import PartitionSpec as P

TILE = 32
OTILES = 4
SQUARE = TILE * TILE
PIECES = 4
STEP_COLS = 256


def lookup(index, table):
    hits = index[:, None] == jnp.arange(table.shape[0], dtype=jnp.int32)[None, :]
    return jnp.sum(
        jnp.where(hits[:, :, None], table[None, :, :], jnp.zeros_like(table)[None, :, :]), axis=1
    )


def symmetry(occ_irrep, vir_irrep, pair_tiles, spin_mask):
    first = lookup(pair_tiles[:, 0], vir_irrep[:, None])[:, 0]
    second = lookup(pair_tiles[:, 1], vir_irrep[:, None])[:, 0]
    pair_irrep = jnp.bitwise_xor(first, second)
    occ_pair = jnp.bitwise_xor(occ_irrep[:, None], occ_irrep[None, :]).reshape(-1)
    allowed = jnp.where(
        (occ_pair[:, None] == pair_irrep[None, :]) & (spin_mask == 1), 1.0, 0.0
    ).astype(jnp.float32)
    coupled = jnp.where(pair_irrep[:, None] == pair_irrep[None, :], 1.0, 0.0).astype(jnp.float32)
    return (allowed, coupled)


def dense_device(
    amplitudes,
    integrals,
    other_terms,
    occ_irrep,
    vir_irrep,
    pair_tiles,
    spin_mask,
    occ_energy,
    vir_energy,
):
    allowed, coupled = symmetry(occ_irrep, vir_irrep, pair_tiles, spin_mask)
    height = amplitudes.shape[0]
    width = amplitudes.shape[1]
    slab_height = integrals.shape[0]
    row_global = lax.axis_index("occ") * height + jnp.arange(height, dtype=jnp.int32)
    col_global = lax.axis_index("vir") * width + jnp.arange(width, dtype=jnp.int32)
    row_block = row_global // SQUARE
    col_pair = col_global // SQUARE
    row_allowed = lookup(row_block, allowed)
    amp_keep = lookup(col_pair, row_allowed.T).T
    masked_amp = jnp.where(amp_keep > 0.5, amplitudes, jnp.zeros_like(amplitudes))
    slab_pair = (
        lax.axis_index("occ") * slab_height + jnp.arange(slab_height, dtype=jnp.int32)
    ) // SQUARE
    int_keep = lookup(col_pair, lookup(slab_pair, coupled).T).T
    masked_slab = jnp.where(int_keep > 0.5, integrals, jnp.zeros_like(integrals))
    whole_amp = lax.all_gather(masked_amp, "vir", axis=1, tiled=True)
    whole_slab = lax.all_gather(masked_slab, "occ", axis=0, tiled=True)
    ladder = jnp.dot(whole_amp, whole_slab, preferred_element_type=jnp.float32)
    inner = row_global % SQUARE
    occ_first = row_block // OTILES * TILE + inner // TILE
    occ_second = row_block % OTILES * TILE + inner % TILE
    occ_sum = (
        lookup(occ_first, occ_energy[:, None])[:, 0] + lookup(occ_second, occ_energy[:, None])[:, 0]
    )
    col_inner = col_global % SQUARE
    tile_first = lookup(col_pair, pair_tiles[:, 0:1])[:, 0]
    tile_second = lookup(col_pair, pair_tiles[:, 1:2])[:, 0]
    vir_first = tile_first * TILE + col_inner // TILE
    vir_second = tile_second * TILE + col_inner % TILE
    vir_sum = (
        lookup(vir_first, vir_energy[:, None])[:, 0] + lookup(vir_second, vir_energy[:, None])[:, 0]
    )
    denom = occ_sum[:, None] - vir_sum[None, :]
    updated = amp_keep * ((ladder + other_terms.astype(jnp.float32)) / denom)
    return updated.astype(jnp.bfloat16)


def pack_kernel(index_ref, block_ref, slot_ref):
    slot_ref[0, 0] = block_ref[...]


def pack(index, place, array, slots, shape):
    half = SQUARE // 2
    return pl.pallas_call(
        pack_kernel,
        out_shape=jax.ShapeDtypeStruct(shape + (SQUARE, SQUARE), array.dtype),
        grid_spec=pltpu.PrefetchScalarGridSpec(
            num_scalar_prefetch=1,
            grid=(slots, 2),
            in_specs=[
                pl.BlockSpec((half, SQUARE), lambda j, r, ix: (ix[j] // 2 * 2 + r, ix[j] % 2))
            ],
            out_specs=pl.BlockSpec(
                (1, 1, half, SQUARE), lambda j, r, ix: (ix[index.shape[0]], j, r, 0)
            ),
        ),
        name="pack",
    )(jnp.concatenate([index, place[None]]), array)


def exchange_kernel(
    n, cap_a, cap_b, a_in, b_in, ag_ref, bg_ref, a_send, a_recv, b_send, b_recv
):
    o = lax.axis_index("occ")
    v = lax.axis_index("vir")

    def place(pos):
        late = pos // (n // 2)
        return 2 * pos * (1 - late) + (2 * (n - 1 - pos) + 1) * late

    odd = o % 2
    pos = (o // 2) * (1 - odd) + (n - 1 - o // 2) * odd
    right = place((pos + 1) % n)
    left = place((pos + n - 1) % n)
    mate = v + 1 - 2 * (v % 2)
    across = (v + 2) % 4
    mesh_id = pl.DeviceIdType.MESH

    barrier = pltpu.get_barrier_semaphore()
    for target in ((right, v), (left, v), (o, mate), (o, across)):
        pl.semaphore_signal(barrier, inc=1, device_id=target, device_id_type=mesh_id)
    pl.semaphore_wait(barrier, 4)

    def a_copy(which, owner, target):
        return pltpu.make_async_remote_copy(
            src_ref=ag_ref.at[owner, pl.ds(0, cap_a)],
            dst_ref=ag_ref.at[owner, pl.ds(0, cap_a)],
            send_sem=a_send.at[which],
            recv_sem=a_recv.at[which],
            device_id=(o, target),
            device_id_type=mesh_id,
        )

    rows = SQUARE // PIECES

    def b_copy(step, piece):
        cut = pl.ds(piece * rows, rows)
        if piece < PIECES // 2:
            owner, target = place((pos + n - step) % n), right
        else:
            owner, target = place((pos + step) % n), left
        return pltpu.make_async_remote_copy(
            src_ref=bg_ref.at[owner, pl.ds(0, cap_b), cut],
            dst_ref=bg_ref.at[owner, pl.ds(0, cap_b), cut],
            send_sem=b_send.at[step, piece],
            recv_sem=b_recv.at[step, piece],
            device_id=(target, v),
            device_id_type=mesh_id,
        )

    order = [p for pair in zip(range(PIECES // 2), range(PIECES // 2, PIECES)) for p in pair]
    b_copies = {}
    for piece in order:
        b_copies[0, piece] = b_copy(0, piece)
        b_copies[0, piece].start()
    to_across = a_copy(0, v, across)
    to_across.start()
    to_mate = a_copy(1, v, mate)
    to_mate.start()
    for step in range(1, n - 1):
        for piece in order:
            b_copies[step - 1, piece].wait_recv()
            b_copies[step, piece] = b_copy(step, piece)
            b_copies[step, piece].start()
    to_across.wait_recv()
    forward = a_copy(2, across, mate)
    forward.start()
    for piece in order:
        b_copies[n - 2, piece].wait_recv()
    to_mate.wait_recv()
    forward.wait_recv()
    for step in range(n - 1):
        for piece in order:
            b_copies[step, piece].wait_send()
    to_across.wait_send()
    to_mate.wait_send()
    forward.wait_send()


def exchange(n, which, cap_a, cap_b, amplitudes, integrals, a_index, b_index):
    packed_a = pack(a_index, lax.axis_index("vir"), amplitudes, cap_a, (4, 4))
    packed_b = pack(b_index, lax.axis_index("occ"), integrals, cap_b, (n, 2))
    any_spec = pl.BlockSpec(memory_space=pl.ANY)
    return pl.pallas_call(
        functools.partial(exchange_kernel, n, cap_a, cap_b),
        out_shape=(
            jax.ShapeDtypeStruct((4, 4, SQUARE, SQUARE), amplitudes.dtype),
            jax.ShapeDtypeStruct((n, 2, SQUARE, SQUARE), integrals.dtype),
        ),
        in_specs=[any_spec, any_spec],
        out_specs=(any_spec, any_spec),
        scratch_shapes=[
            pltpu.SemaphoreType.DMA((3,)),
            pltpu.SemaphoreType.DMA((3,)),
            pltpu.SemaphoreType.DMA((n - 1, PIECES)),
            pltpu.SemaphoreType.DMA((n - 1, PIECES)),
        ],
        input_output_aliases={0: 0, 1: 1},
        compiler_params=pltpu.CompilerParams(collective_id=which, has_side_effects=True),
        name="exchange",
    )(packed_a, packed_b)


def ladder_kernel(
    count_ref, keep_ref, a_slot, b_slot, a_ref, b_ref, other_ref, occ_ref, vir_ref, out_ref, acc
):
    block = pl.program_id(0)
    step = pl.program_id(1)
    count = count_ref[block]
    a_block = a_ref.at[0]
    b_block = b_ref.at[0]

    @pl.when(step == 0)
    def _():
        acc[...] = jnp.zeros_like(acc)

    @pl.when(step < count)
    def _():
        @pl.loop(0, SQUARE // STEP_COLS)
        def _(part):
            cols = pl.ds(pl.multiple_of(part * STEP_COLS, STEP_COLS), STEP_COLS)
            acc[:, cols] += jnp.dot(
                a_block[...], b_block[:, cols], preferred_element_type=jnp.float32
            )

    last = step == pl.num_programs(1) - 1

    @pl.when(last & (keep_ref[block] == 1))
    def _():
        @pl.loop(0, SQUARE // 128)
        def _(part):
            cut = pl.ds(pl.multiple_of(part * 128, 128), 128)
            denom = occ_ref[0, cut, :] - vir_ref[0]
            total = acc[cut, :] + other_ref[cut, :].astype(jnp.float32)
            out_ref[cut, :] = (total / denom).astype(out_ref.dtype)

    @pl.when(last & (keep_ref[block] == 0))
    def _():
        out_ref[...] = jnp.zeros_like(out_ref)


def ladder(count, keep, a_slot, b_slot, steps, a_all, b_all, other_terms, occ_sum, vir_sum):
    square = (SQUARE, SQUARE)
    return pl.pallas_call(
        ladder_kernel,
        out_shape=jax.ShapeDtypeStruct(other_terms.shape, other_terms.dtype),
        grid_spec=pltpu.PrefetchScalarGridSpec(
            num_scalar_prefetch=4,
            grid=(4, steps),
            in_specs=[
                pl.BlockSpec((1,) + square, lambda b, j, c, k, sa, sb: (sa[b * steps + j], 0, 0)),
                pl.BlockSpec((1,) + square, lambda b, j, c, k, sa, sb: (sb[b * steps + j], 0, 0)),
                pl.BlockSpec(square, lambda b, j, c, k, sa, sb: (b // 2, b % 2)),
                pl.BlockSpec((1, SQUARE, 1), lambda b, j, c, k, sa, sb: (b // 2, 0, 0)),
                pl.BlockSpec((1, 1, SQUARE), lambda b, j, c, k, sa, sb: (b % 2, 0, 0)),
            ],
            out_specs=pl.BlockSpec(square, lambda b, j, c, k, sa, sb: (b // 2, b % 2)),
            scratch_shapes=[pltpu.VMEM(square, jnp.float32)],
        ),
        compiler_params=pltpu.CompilerParams(vmem_limit_bytes=48 << 20),
        name="ladder",
    )(count, keep, a_slot, b_slot, a_all, b_all, other_terms, occ_sum, vir_sum)


def ranks(flags):
    size = flags.shape[-1]
    before = jnp.arange(size)[:, None] < jnp.arange(size)[None, :]
    return jnp.sum(jnp.where(before, flags[..., :, None], 0), axis=-2)


def pick(flags, rank, values, size):
    total = jnp.sum(flags, axis=-1, keepdims=True)
    want = jnp.minimum(jnp.arange(size), jnp.maximum(total - 1, 0))
    hit = (flags[..., :, None] == 1) & (rank[..., :, None] == want[..., None, :])
    return jnp.sum(jnp.where(hit, values[..., :, None], 0), axis=-2)


def block_device(
    amplitudes,
    integrals,
    other_terms,
    occ_irrep,
    vir_irrep,
    pair_tiles,
    spin_mask,
    occ_energy,
    vir_energy,
):
    o = lax.axis_index("occ")
    v = lax.axis_index("vir")
    allowed, _ = symmetry(occ_irrep, vir_irrep, pair_tiles, spin_mask)
    allowed = allowed.astype(jnp.int32)
    pairs = allowed.shape[1]
    occ_devices = allowed.shape[0] // 2
    used = jnp.max(allowed[:, :, None] * allowed[:, None, :], axis=0)
    a_flags = allowed.reshape(occ_devices, 2, 4, 2).transpose(0, 2, 1, 3).reshape(occ_devices, 4, 4)
    b_flags = used.reshape(pairs, 4, 2)
    a_most = jnp.max(jnp.sum(a_flags, axis=-1))
    b_most = jnp.max(jnp.sum(b_flags, axis=-1))

    a_here = lax.dynamic_index_in_dim(a_flags, o, 0, keepdims=False)
    a_rank = ranks(a_here)
    b_here = lax.dynamic_index_in_dim(b_flags, v, 1, keepdims=False)
    b_rank = ranks(b_here)
    a_mine = lax.dynamic_index_in_dim(a_here, v, 0, keepdims=False)
    b_mine = lax.dynamic_index_in_dim(b_here, o, 0, keepdims=False)
    a_index = pick(a_mine, ranks(a_mine), jnp.arange(4, dtype=jnp.int32), 4)
    b_index = pick(b_mine, ranks(b_mine), jnp.arange(2, dtype=jnp.int32), 2)

    variant = jnp.where(b_most > 1, 2, jnp.where(a_most > 2, 1, 0))
    run = functools.partial(exchange, occ_devices)
    a_all, b_all = lax.switch(
        variant,
        [
            functools.partial(run, 0, 2, 1),
            functools.partial(run, 1, 4, 1),
            functools.partial(run, 2, 4, 2),
        ],
        amplitudes,
        integrals,
        a_index,
        b_index,
    )

    a_rows = a_here.reshape(4, 2, 2).transpose(1, 0, 2).reshape(2, pairs)
    a_at = (a_rank + 4 * jnp.arange(4, dtype=jnp.int32)[:, None]).reshape(4, 2, 2)
    a_at = a_at.transpose(1, 0, 2).reshape(2, pairs)
    b_at = (b_rank + 2 * jnp.arange(pairs, dtype=jnp.int32)[:, None]).T
    keep = a_mine.reshape(2, 2)
    terms = a_rows[:, None, :] * keep[:, :, None]
    order = ranks(terms)
    a_slot = pick(terms, order, jnp.broadcast_to(a_at[:, None, :], terms.shape), pairs)
    b_slot = pick(terms, order, jnp.broadcast_to(b_at[None, :, :], terms.shape), pairs)
    count = jnp.sum(terms, axis=-1).reshape(-1)

    occ_tiles = occ_energy.reshape(OTILES, TILE)
    pair_occ = (occ_tiles[:, None, :, None] + occ_tiles[None, :, None, :]).reshape(-1, SQUARE)
    occ_sum = lax.dynamic_slice_in_dim(pair_occ, 2 * o, 2, 0)[:, :, None]
    vir_tiles = vir_energy.reshape(-1, TILE)
    tiles = lax.dynamic_slice_in_dim(pair_tiles, 2 * v, 2, 0)
    first = lookup(tiles[:, 0], vir_tiles)
    second = lookup(tiles[:, 1], vir_tiles)
    vir_sum = (first[:, :, None] + second[:, None, :]).reshape(2, 1, SQUARE)

    return ladder(
        count,
        keep.reshape(-1),
        a_slot.reshape(-1),
        b_slot.reshape(-1),
        pairs,
        a_all.reshape(-1, SQUARE, SQUARE),
        b_all.reshape(-1, SQUARE, SQUARE),
        other_terms,
        occ_sum,
        vir_sum,
    )


def per_device(amplitudes, integrals, *rest):
    blocks = amplitudes.shape == (2 * SQUARE, 2 * SQUARE)
    blocks = blocks and integrals.shape == (SQUARE, 2 * SQUARE) and lax.axis_size("vir") == 4
    blocks = blocks and lax.axis_size("occ") == OTILES * OTILES // 2
    device = block_device if blocks else dense_device
    return device(amplitudes, integrals, *rest)


def solution(mesh):
    in_specs = (P("occ", "vir"), P("occ", "vir"), P("occ", "vir"), P(), P(), P(), P(), P(), P())
    out_specs = P("occ", "vir")
    return jax.shard_map(
        per_device, mesh=mesh, in_specs=in_specs, out_specs=out_specs, check_vma=False
    )
```

```python
import functools

import jax
import jax.numpy as jnp
from jax import lax
from jax.experimental import pallas as pl
from jax.experimental.pallas import tpu as pltpu
from jax.sharding import PartitionSpec as P

TILE = 32
OTILES = 4
SQUARE = TILE * TILE
PIECES = 4
STEP_COLS = 256


def lookup(index, table):
    hits = index[:, None] == jnp.arange(table.shape[0], dtype=jnp.int32)[None, :]
    return jnp.sum(
        jnp.where(hits[:, :, None], table[None, :, :], jnp.zeros_like(table)[None, :, :]), axis=1
    )


def symmetry(occ_irrep, vir_irrep, pair_tiles, spin_mask):
    first = lookup(pair_tiles[:, 0], vir_irrep[:, None])[:, 0]
    second = lookup(pair_tiles[:, 1], vir_irrep[:, None])[:, 0]
    pair_irrep = jnp.bitwise_xor(first, second)
    occ_pair = jnp.bitwise_xor(occ_irrep[:, None], occ_irrep[None, :]).reshape(-1)
    allowed = jnp.where(
        (occ_pair[:, None] == pair_irrep[None, :]) & (spin_mask == 1), 1.0, 0.0
    ).astype(jnp.float32)
    coupled = jnp.where(pair_irrep[:, None] == pair_irrep[None, :], 1.0, 0.0).astype(jnp.float32)
    return (allowed, coupled)


def dense_device(
    amplitudes,
    integrals,
    other_terms,
    occ_irrep,
    vir_irrep,
    pair_tiles,
    spin_mask,
    occ_energy,
    vir_energy,
):
    allowed, coupled = symmetry(occ_irrep, vir_irrep, pair_tiles, spin_mask)
    height = amplitudes.shape[0]
    width = amplitudes.shape[1]
    slab_height = integrals.shape[0]
    row_global = lax.axis_index("occ") * height + jnp.arange(height, dtype=jnp.int32)
    col_global = lax.axis_index("vir") * width + jnp.arange(width, dtype=jnp.int32)
    row_block = row_global // SQUARE
    col_pair = col_global // SQUARE
    row_allowed = lookup(row_block, allowed)
    amp_keep = lookup(col_pair, row_allowed.T).T
    masked_amp = jnp.where(amp_keep > 0.5, amplitudes, jnp.zeros_like(amplitudes))
    slab_pair = (
        lax.axis_index("occ") * slab_height + jnp.arange(slab_height, dtype=jnp.int32)
    ) // SQUARE
    int_keep = lookup(col_pair, lookup(slab_pair, coupled).T).T
    masked_slab = jnp.where(int_keep > 0.5, integrals, jnp.zeros_like(integrals))
    whole_amp = lax.all_gather(masked_amp, "vir", axis=1, tiled=True)
    whole_slab = lax.all_gather(masked_slab, "occ", axis=0, tiled=True)
    ladder = jnp.dot(whole_amp, whole_slab, preferred_element_type=jnp.float32)
    inner = row_global % SQUARE
    occ_first = row_block // OTILES * TILE + inner // TILE
    occ_second = row_block % OTILES * TILE + inner % TILE
    occ_sum = (
        lookup(occ_first, occ_energy[:, None])[:, 0] + lookup(occ_second, occ_energy[:, None])[:, 0]
    )
    col_inner = col_global % SQUARE
    tile_first = lookup(col_pair, pair_tiles[:, 0:1])[:, 0]
    tile_second = lookup(col_pair, pair_tiles[:, 1:2])[:, 0]
    vir_first = tile_first * TILE + col_inner // TILE
    vir_second = tile_second * TILE + col_inner % TILE
    vir_sum = (
        lookup(vir_first, vir_energy[:, None])[:, 0] + lookup(vir_second, vir_energy[:, None])[:, 0]
    )
    denom = occ_sum[:, None] - vir_sum[None, :]
    updated = amp_keep * ((ladder + other_terms.astype(jnp.float32)) / denom)
    return updated.astype(jnp.bfloat16)


def pack_kernel(index_ref, block_ref, slot_ref):
    slot_ref[0, 0] = block_ref[...]


def pack(index, place, array, slots, shape):
    half = SQUARE // 2
    return pl.pallas_call(
        pack_kernel,
        out_shape=jax.ShapeDtypeStruct(shape + (SQUARE, SQUARE), array.dtype),
        grid_spec=pltpu.PrefetchScalarGridSpec(
            num_scalar_prefetch=1,
            grid=(slots, 2),
            in_specs=[
                pl.BlockSpec((half, SQUARE), lambda j, r, ix: (ix[j] // 2 * 2 + r, ix[j] % 2))
            ],
            out_specs=pl.BlockSpec(
                (1, 1, half, SQUARE), lambda j, r, ix: (ix[index.shape[0]], j, r, 0)
            ),
        ),
        name="pack",
    )(jnp.concatenate([index, place[None]]), array)


def exchange_kernel(
    n, cap_a, window, a_in, b_in, ag_ref, bg_ref, a_send, a_recv, b_send, b_recv
):
    o = lax.axis_index("occ")
    v = lax.axis_index("vir")

    def place(pos):
        late = pos // (n // 2)
        return 2 * pos * (1 - late) + (2 * (n - 1 - pos) + 1) * late

    odd = o % 2
    pos = (o // 2) * (1 - odd) + (n - 1 - o // 2) * odd
    right = place((pos + 1) % n)
    left = place((pos + n - 1) % n)
    mate = v + 1 - 2 * (v % 2)
    across = (v + 2) % 4
    mesh_id = pl.DeviceIdType.MESH

    barrier = pltpu.get_barrier_semaphore()
    for target in ((right, v), (left, v), (o, mate), (o, across)):
        pl.semaphore_signal(barrier, inc=1, device_id=target, device_id_type=mesh_id)
    pl.semaphore_wait(barrier, 4)

    def a_copy(which, owner, target):
        return pltpu.make_async_remote_copy(
            src_ref=ag_ref.at[owner, pl.ds(0, cap_a)],
            dst_ref=ag_ref.at[owner, pl.ds(0, cap_a)],
            send_sem=a_send.at[which],
            recv_sem=a_recv.at[which],
            device_id=(o, target),
            device_id_type=mesh_id,
        )

    def b_copy(step, piece):
        if piece < PIECES // 2:
            owner, target = place((pos + n - step) % n), right
        else:
            owner, target = place((pos + step) % n), left
        return pltpu.make_async_remote_copy(
            src_ref=window(bg_ref, owner, piece),
            dst_ref=window(bg_ref, owner, piece),
            send_sem=b_send.at[step, piece],
            recv_sem=b_recv.at[step, piece],
            device_id=(target, v),
            device_id_type=mesh_id,
        )

    order = [p for pair in zip(range(PIECES // 2), range(PIECES // 2, PIECES)) for p in pair]
    b_copies = {}
    for piece in order:
        b_copies[0, piece] = b_copy(0, piece)
        b_copies[0, piece].start()
    to_across = a_copy(0, v, across)
    to_across.start()
    to_mate = a_copy(1, v, mate)
    to_mate.start()
    for step in range(1, n - 1):
        for piece in order:
            b_copies[step - 1, piece].wait_recv()
            b_copies[step, piece] = b_copy(step, piece)
            b_copies[step, piece].start()
    to_across.wait_recv()
    forward = a_copy(2, across, mate)
    forward.start()
    for piece in order:
        b_copies[n - 2, piece].wait_recv()
    to_mate.wait_recv()
    forward.wait_recv()
    for step in range(n - 1):
        for piece in order:
            b_copies[step, piece].wait_send()
    to_across.wait_send()
    to_mate.wait_send()
    forward.wait_send()


def slot_window(cap_b, ref, owner, piece):
    rows = SQUARE // PIECES
    return ref.at[owner, pl.ds(0, cap_b), pl.ds(piece * rows, rows)]


def slice_window(n, slots, ref, owner, piece):
    rows = SQUARE // n // PIECES
    start = pl.multiple_of(owner * (SQUARE // n) + piece * rows, rows)
    return ref.at[pl.ds(0, slots), pl.ds(start, rows)]


def exchange(n, which, cap_a, window, amps, ints):
    any_spec = pl.BlockSpec(memory_space=pl.ANY)
    return pl.pallas_call(
        functools.partial(exchange_kernel, n, cap_a, window),
        out_shape=(
            jax.ShapeDtypeStruct(amps.shape, amps.dtype),
            jax.ShapeDtypeStruct(ints.shape, ints.dtype),
        ),
        in_specs=[any_spec, any_spec],
        out_specs=(any_spec, any_spec),
        scratch_shapes=[
            pltpu.SemaphoreType.DMA((3,)),
            pltpu.SemaphoreType.DMA((3,)),
            pltpu.SemaphoreType.DMA((n - 1, PIECES)),
            pltpu.SemaphoreType.DMA((n - 1, PIECES)),
        ],
        input_output_aliases={0: 0, 1: 1},
        compiler_params=pltpu.CompilerParams(collective_id=which, has_side_effects=True),
        name="exchange",
    )(amps, ints)


def spread_kernel(n, b_ref, out_ref, own_sem, send_sem, recv_sem):
    o = lax.axis_index("occ")
    v = lax.axis_index("vir")
    mesh_id = pl.DeviceIdType.MESH
    rows = SQUARE // n

    def part(owner):
        return b_ref.at[pl.ds(pl.multiple_of(owner * rows, rows), rows)]

    barrier = pltpu.get_barrier_semaphore()
    for away in range(1, n):
        pl.semaphore_signal(
            barrier, inc=1, device_id=((o + away) % n, v), device_id_type=mesh_id
        )
    pl.semaphore_wait(barrier, n - 1)
    copies = []
    for away in range(1, n):
        target = (o + away) % n
        copies.append(
            pltpu.make_async_remote_copy(
                src_ref=part(target),
                dst_ref=out_ref.at[o],
                send_sem=send_sem.at[away - 1],
                recv_sem=recv_sem.at[away - 1],
                device_id=(target, v),
                device_id_type=mesh_id,
            )
        )
        copies[-1].start()
    own = pltpu.make_async_copy(part(o), out_ref.at[o], own_sem)
    own.start()
    for copy in copies:
        copy.wait_recv()
    for copy in copies:
        copy.wait_send()
    own.wait()


def spread(n, which, integrals):
    any_spec = pl.BlockSpec(memory_space=pl.ANY)
    return pl.pallas_call(
        functools.partial(spread_kernel, n),
        out_shape=jax.ShapeDtypeStruct((n, SQUARE // n, 2 * SQUARE), integrals.dtype),
        in_specs=[any_spec],
        out_specs=any_spec,
        scratch_shapes=[
            pltpu.SemaphoreType.DMA,
            pltpu.SemaphoreType.DMA((n - 1,)),
            pltpu.SemaphoreType.DMA((n - 1,)),
        ],
        compiler_params=pltpu.CompilerParams(collective_id=which, has_side_effects=True),
        name="spread",
    )(integrals)


def select_kernel(index_ref, part_ref, slot_ref):
    slot_ref[...] = part_ref[...]


def select(index, place, parts, slots):
    n, rows = parts.shape[:2]
    last = index.shape[0]
    return pl.pallas_call(
        select_kernel,
        out_shape=jax.ShapeDtypeStruct((2 * n, SQUARE, SQUARE), parts.dtype),
        grid_spec=pltpu.PrefetchScalarGridSpec(
            num_scalar_prefetch=1,
            grid=(slots,),
            in_specs=[pl.BlockSpec((1, rows, SQUARE), lambda j, ix: (ix[j] // 2, 0, ix[j] % 2))],
            out_specs=pl.BlockSpec((1, rows, SQUARE), lambda j, ix: (j, ix[last], 0)),
        ),
        name="select",
    )(jnp.concatenate([index, place[None]]), parts)


def by_slots(n, which, cap_a, cap_b, amplitudes, integrals, a_index, b_index, all_index):
    amps = pack(a_index, lax.axis_index("vir"), amplitudes, cap_a, (4, 4))
    ints = pack(b_index, lax.axis_index("occ"), integrals, cap_b, (n, 2))
    window = functools.partial(slot_window, cap_b)
    amps, ints = exchange(n, which, cap_a, window, amps, ints)
    return amps, ints.reshape(2 * n, SQUARE, SQUARE)


def by_slices(n, which, cap_a, slots, amplitudes, integrals, a_index, b_index, all_index):
    parts = spread(n, which, integrals)
    amps = pack(a_index, lax.axis_index("vir"), amplitudes, cap_a, (4, 4))
    ints = select(all_index, lax.axis_index("occ"), parts, slots)
    window = functools.partial(slice_window, n, slots)
    return exchange(n, which + 1, cap_a, window, amps, ints)


def ladder_kernel(
    count_ref, keep_ref, a_slot, b_slot, a_ref, b_ref, other_ref, occ_ref, vir_ref, out_ref, acc
):
    block = pl.program_id(0)
    step = pl.program_id(1)
    count = count_ref[block]
    a_block = a_ref.at[0]
    b_block = b_ref.at[0]

    @pl.when(step == 0)
    def _():
        acc[...] = jnp.zeros_like(acc)

    @pl.when(step < count)
    def _():
        @pl.loop(0, SQUARE // STEP_COLS)
        def _(part):
            cols = pl.ds(pl.multiple_of(part * STEP_COLS, STEP_COLS), STEP_COLS)
            acc[:, cols] += jnp.dot(
                a_block[...], b_block[:, cols], preferred_element_type=jnp.float32
            )

    last = step == pl.num_programs(1) - 1

    @pl.when(last & (keep_ref[block] == 1))
    def _():
        @pl.loop(0, SQUARE // 128)
        def _(part):
            cut = pl.ds(pl.multiple_of(part * 128, 128), 128)
            denom = occ_ref[0, cut, :] - vir_ref[0]
            total = acc[cut, :] + other_ref[cut, :].astype(jnp.float32)
            out_ref[cut, :] = (total / denom).astype(out_ref.dtype)

    @pl.when(last & (keep_ref[block] == 0))
    def _():
        out_ref[...] = jnp.zeros_like(out_ref)


def ladder(count, keep, a_slot, b_slot, steps, a_all, b_all, other_terms, occ_sum, vir_sum):
    square = (SQUARE, SQUARE)
    return pl.pallas_call(
        ladder_kernel,
        out_shape=jax.ShapeDtypeStruct(other_terms.shape, other_terms.dtype),
        grid_spec=pltpu.PrefetchScalarGridSpec(
            num_scalar_prefetch=4,
            grid=(4, steps),
            in_specs=[
                pl.BlockSpec((1,) + square, lambda b, j, c, k, sa, sb: (sa[b * steps + j], 0, 0)),
                pl.BlockSpec((1,) + square, lambda b, j, c, k, sa, sb: (sb[b * steps + j], 0, 0)),
                pl.BlockSpec(square, lambda b, j, c, k, sa, sb: (b // 2, b % 2)),
                pl.BlockSpec((1, SQUARE, 1), lambda b, j, c, k, sa, sb: (b // 2, 0, 0)),
                pl.BlockSpec((1, 1, SQUARE), lambda b, j, c, k, sa, sb: (b % 2, 0, 0)),
            ],
            out_specs=pl.BlockSpec(square, lambda b, j, c, k, sa, sb: (b // 2, b % 2)),
            scratch_shapes=[pltpu.VMEM(square, jnp.float32)],
        ),
        compiler_params=pltpu.CompilerParams(vmem_limit_bytes=48 << 20),
        name="ladder",
    )(count, keep, a_slot, b_slot, a_all, b_all, other_terms, occ_sum, vir_sum)


def ranks(flags):
    size = flags.shape[-1]
    before = jnp.arange(size)[:, None] < jnp.arange(size)[None, :]
    return jnp.sum(jnp.where(before, flags[..., :, None], 0), axis=-2)


def pick(flags, rank, values, size):
    total = jnp.sum(flags, axis=-1, keepdims=True)
    want = jnp.minimum(jnp.arange(size), jnp.maximum(total - 1, 0))
    hit = (flags[..., :, None] == 1) & (rank[..., :, None] == want[..., None, :])
    return jnp.sum(jnp.where(hit, values[..., :, None], 0), axis=-2)


def block_device(
    amplitudes,
    integrals,
    other_terms,
    occ_irrep,
    vir_irrep,
    pair_tiles,
    spin_mask,
    occ_energy,
    vir_energy,
):
    o = lax.axis_index("occ")
    v = lax.axis_index("vir")
    allowed, _ = symmetry(occ_irrep, vir_irrep, pair_tiles, spin_mask)
    allowed = allowed.astype(jnp.int32)
    pairs = allowed.shape[1]
    occ_devices = allowed.shape[0] // 2
    used = jnp.max(allowed[:, :, None] * allowed[:, None, :], axis=0)
    a_flags = allowed.reshape(occ_devices, 2, 4, 2).transpose(0, 2, 1, 3).reshape(occ_devices, 4, 4)
    b_flags = used.reshape(pairs, 4, 2)
    a_most = jnp.max(jnp.sum(a_flags, axis=-1))
    b_most = jnp.max(jnp.sum(b_flags, axis=-1))

    a_here = lax.dynamic_index_in_dim(a_flags, o, 0, keepdims=False)
    a_rank = ranks(a_here)
    b_here = lax.dynamic_index_in_dim(b_flags, v, 1, keepdims=False)
    b_rank = ranks(b_here)
    a_mine = lax.dynamic_index_in_dim(a_here, v, 0, keepdims=False)
    b_mine = lax.dynamic_index_in_dim(b_here, o, 0, keepdims=False)
    a_index = pick(a_mine, ranks(a_mine), jnp.arange(4, dtype=jnp.int32), 4)
    b_index = pick(b_mine, ranks(b_mine), jnp.arange(2, dtype=jnp.int32), 2)

    all_flags = b_here.reshape(-1)
    all_rank = ranks(all_flags)
    all_index = pick(all_flags, all_rank, jnp.arange(2 * pairs, dtype=jnp.int32), 8)
    all_most = jnp.max(jnp.sum(b_flags, axis=(0, 2)))

    wide = (a_most > 2).astype(jnp.int32)
    sliced = (b_most > 1) & (all_most <= 8)
    by_slice = jnp.where((all_most <= 6) & (a_most <= 2), 3, 4 + wide)
    variant = jnp.where(sliced, by_slice, jnp.where(b_most > 1, 2, wide))
    slots = functools.partial(by_slots, occ_devices)
    slices = functools.partial(by_slices, occ_devices)
    a_all, b_all = lax.switch(
        variant,
        [
            functools.partial(slots, 0, 2, 1),
            functools.partial(slots, 1, 4, 1),
            functools.partial(slots, 2, 4, 2),
            functools.partial(slices, 3, 2, 6),
            functools.partial(slices, 5, 2, 8),
            functools.partial(slices, 7, 4, 8),
        ],
        amplitudes,
        integrals,
        a_index,
        b_index,
        all_index,
    )

    a_rows = a_here.reshape(4, 2, 2).transpose(1, 0, 2).reshape(2, pairs)
    a_at = (a_rank + 4 * jnp.arange(4, dtype=jnp.int32)[:, None]).reshape(4, 2, 2)
    a_at = a_at.transpose(1, 0, 2).reshape(2, pairs)
    b_at = b_rank + 2 * jnp.arange(pairs, dtype=jnp.int32)[:, None]
    b_at = jnp.where(sliced, all_rank.reshape(pairs, 2), b_at).T
    keep = a_mine.reshape(2, 2)
    terms = a_rows[:, None, :] * keep[:, :, None]
    order = ranks(terms)
    a_slot = pick(terms, order, jnp.broadcast_to(a_at[:, None, :], terms.shape), pairs)
    b_slot = pick(terms, order, jnp.broadcast_to(b_at[None, :, :], terms.shape), pairs)
    count = jnp.sum(terms, axis=-1).reshape(-1)

    occ_tiles = occ_energy.reshape(OTILES, TILE)
    pair_occ = (occ_tiles[:, None, :, None] + occ_tiles[None, :, None, :]).reshape(-1, SQUARE)
    occ_sum = lax.dynamic_slice_in_dim(pair_occ, 2 * o, 2, 0)[:, :, None]
    vir_tiles = vir_energy.reshape(-1, TILE)
    tiles = lax.dynamic_slice_in_dim(pair_tiles, 2 * v, 2, 0)
    first = lookup(tiles[:, 0], vir_tiles)
    second = lookup(tiles[:, 1], vir_tiles)
    vir_sum = (first[:, :, None] + second[:, None, :]).reshape(2, 1, SQUARE)

    return ladder(
        count,
        keep.reshape(-1),
        a_slot.reshape(-1),
        b_slot.reshape(-1),
        pairs,
        a_all.reshape(-1, SQUARE, SQUARE),
        b_all,
        other_terms,
        occ_sum,
        vir_sum,
    )


def per_device(amplitudes, integrals, *rest):
    blocks = amplitudes.shape == (2 * SQUARE, 2 * SQUARE)
    blocks = blocks and integrals.shape == (SQUARE, 2 * SQUARE) and lax.axis_size("vir") == 4
    blocks = blocks and lax.axis_size("occ") == OTILES * OTILES // 2
    device = block_device if blocks else dense_device
    return device(amplitudes, integrals, *rest)


def solution(mesh):
    in_specs = (P("occ", "vir"), P("occ", "vir"), P("occ", "vir"), P(), P(), P(), P(), P(), P())
    out_specs = P("occ", "vir")
    return jax.shard_map(
        per_device, mesh=mesh, in_specs=in_specs, out_specs=out_specs, check_vma=False
    )
```

```python
import functools

import jax
import jax.numpy as jnp
from jax import lax
from jax.experimental import pallas as pl
from jax.experimental.pallas import tpu as pltpu
from jax.sharding import PartitionSpec as P

TILE = 32
OTILES = 4
SQUARE = TILE * TILE
PIECES = 4
STEP_COLS = 256


def lookup(index, table):
    hits = index[:, None] == jnp.arange(table.shape[0], dtype=jnp.int32)[None, :]
    return jnp.sum(
        jnp.where(hits[:, :, None], table[None, :, :], jnp.zeros_like(table)[None, :, :]), axis=1
    )


def symmetry(occ_irrep, vir_irrep, pair_tiles, spin_mask):
    first = lookup(pair_tiles[:, 0], vir_irrep[:, None])[:, 0]
    second = lookup(pair_tiles[:, 1], vir_irrep[:, None])[:, 0]
    pair_irrep = jnp.bitwise_xor(first, second)
    occ_pair = jnp.bitwise_xor(occ_irrep[:, None], occ_irrep[None, :]).reshape(-1)
    allowed = jnp.where(
        (occ_pair[:, None] == pair_irrep[None, :]) & (spin_mask == 1), 1.0, 0.0
    ).astype(jnp.float32)
    coupled = jnp.where(pair_irrep[:, None] == pair_irrep[None, :], 1.0, 0.0).astype(jnp.float32)
    return (allowed, coupled)


def dense_device(
    amplitudes,
    integrals,
    other_terms,
    occ_irrep,
    vir_irrep,
    pair_tiles,
    spin_mask,
    occ_energy,
    vir_energy,
):
    allowed, coupled = symmetry(occ_irrep, vir_irrep, pair_tiles, spin_mask)
    height = amplitudes.shape[0]
    width = amplitudes.shape[1]
    slab_height = integrals.shape[0]
    row_global = lax.axis_index("occ") * height + jnp.arange(height, dtype=jnp.int32)
    col_global = lax.axis_index("vir") * width + jnp.arange(width, dtype=jnp.int32)
    row_block = row_global // SQUARE
    col_pair = col_global // SQUARE
    row_allowed = lookup(row_block, allowed)
    amp_keep = lookup(col_pair, row_allowed.T).T
    masked_amp = jnp.where(amp_keep > 0.5, amplitudes, jnp.zeros_like(amplitudes))
    slab_pair = (
        lax.axis_index("occ") * slab_height + jnp.arange(slab_height, dtype=jnp.int32)
    ) // SQUARE
    int_keep = lookup(col_pair, lookup(slab_pair, coupled).T).T
    masked_slab = jnp.where(int_keep > 0.5, integrals, jnp.zeros_like(integrals))
    whole_amp = lax.all_gather(masked_amp, "vir", axis=1, tiled=True)
    whole_slab = lax.all_gather(masked_slab, "occ", axis=0, tiled=True)
    ladder = jnp.dot(whole_amp, whole_slab, preferred_element_type=jnp.float32)
    inner = row_global % SQUARE
    occ_first = row_block // OTILES * TILE + inner // TILE
    occ_second = row_block % OTILES * TILE + inner % TILE
    occ_sum = (
        lookup(occ_first, occ_energy[:, None])[:, 0] + lookup(occ_second, occ_energy[:, None])[:, 0]
    )
    col_inner = col_global % SQUARE
    tile_first = lookup(col_pair, pair_tiles[:, 0:1])[:, 0]
    tile_second = lookup(col_pair, pair_tiles[:, 1:2])[:, 0]
    vir_first = tile_first * TILE + col_inner // TILE
    vir_second = tile_second * TILE + col_inner % TILE
    vir_sum = (
        lookup(vir_first, vir_energy[:, None])[:, 0] + lookup(vir_second, vir_energy[:, None])[:, 0]
    )
    denom = occ_sum[:, None] - vir_sum[None, :]
    updated = amp_keep * ((ladder + other_terms.astype(jnp.float32)) / denom)
    return updated.astype(jnp.bfloat16)


def pack_kernel(index_ref, block_ref, slot_ref):
    slot_ref[0, 0] = block_ref[...]


def pack(index, place, array, slots, shape):
    half = SQUARE // 2
    return pl.pallas_call(
        pack_kernel,
        out_shape=jax.ShapeDtypeStruct(shape + (SQUARE, SQUARE), array.dtype),
        grid_spec=pltpu.PrefetchScalarGridSpec(
            num_scalar_prefetch=1,
            grid=(slots, 2),
            in_specs=[
                pl.BlockSpec((half, SQUARE), lambda j, r, ix: (ix[j] // 2 * 2 + r, ix[j] % 2))
            ],
            out_specs=pl.BlockSpec(
                (1, 1, half, SQUARE), lambda j, r, ix: (ix[index.shape[0]], j, r, 0)
            ),
        ),
        name="pack",
    )(jnp.concatenate([index, place[None]]), array)


def exchange_kernel(
    n, cap_a, window, a_in, b_in, ag_ref, bg_ref, a_send, a_recv, b_send, b_recv
):
    o = lax.axis_index("occ")
    v = lax.axis_index("vir")

    def place(pos):
        late = pos // (n // 2)
        return 2 * pos * (1 - late) + (2 * (n - 1 - pos) + 1) * late

    odd = o % 2
    pos = (o // 2) * (1 - odd) + (n - 1 - o // 2) * odd
    right = place((pos + 1) % n)
    left = place((pos + n - 1) % n)
    mate = v + 1 - 2 * (v % 2)
    across = (v + 2) % 4
    mesh_id = pl.DeviceIdType.MESH

    barrier = pltpu.get_barrier_semaphore()
    for target in ((right, v), (left, v), (o, mate), (o, across)):
        pl.semaphore_signal(barrier, inc=1, device_id=target, device_id_type=mesh_id)
    pl.semaphore_wait(barrier, 4)

    def a_copy(which, owner, target):
        return pltpu.make_async_remote_copy(
            src_ref=ag_ref.at[owner, pl.ds(0, cap_a)],
            dst_ref=ag_ref.at[owner, pl.ds(0, cap_a)],
            send_sem=a_send.at[which],
            recv_sem=a_recv.at[which],
            device_id=(o, target),
            device_id_type=mesh_id,
        )

    def b_copy(step, piece):
        if piece < PIECES // 2:
            owner, target = place((pos + n - step) % n), right
        else:
            owner, target = place((pos + step) % n), left
        return pltpu.make_async_remote_copy(
            src_ref=window(bg_ref, owner, piece),
            dst_ref=window(bg_ref, owner, piece),
            send_sem=b_send.at[step, piece],
            recv_sem=b_recv.at[step, piece],
            device_id=(target, v),
            device_id_type=mesh_id,
        )

    order = [p for pair in zip(range(PIECES // 2), range(PIECES // 2, PIECES)) for p in pair]
    b_copies = {}
    for piece in order:
        b_copies[0, piece] = b_copy(0, piece)
        b_copies[0, piece].start()
    to_across = a_copy(0, v, across)
    to_across.start()
    to_mate = a_copy(1, v, mate)
    to_mate.start()
    for step in range(1, n - 1):
        for piece in order:
            b_copies[step - 1, piece].wait_recv()
            b_copies[step, piece] = b_copy(step, piece)
            b_copies[step, piece].start()
    to_across.wait_recv()
    forward = a_copy(2, across, mate)
    forward.start()
    for piece in order:
        b_copies[n - 2, piece].wait_recv()
    to_mate.wait_recv()
    forward.wait_recv()
    for step in range(n - 1):
        for piece in order:
            b_copies[step, piece].wait_send()
    to_across.wait_send()
    to_mate.wait_send()
    forward.wait_send()


def slot_window(cap_b, ref, owner, piece):
    rows = SQUARE // PIECES
    return ref.at[owner, pl.ds(0, cap_b), pl.ds(piece * rows, rows)]


def slice_window(n, slots, ref, owner, piece):
    rows = SQUARE // n // PIECES
    start = pl.multiple_of(owner * (SQUARE // n) + piece * rows, rows)
    return ref.at[pl.ds(0, slots), pl.ds(start, rows)]


def exchange(n, which, cap_a, window, amps, ints):
    any_spec = pl.BlockSpec(memory_space=pl.ANY)
    return pl.pallas_call(
        functools.partial(exchange_kernel, n, cap_a, window),
        out_shape=(
            jax.ShapeDtypeStruct(amps.shape, amps.dtype),
            jax.ShapeDtypeStruct(ints.shape, ints.dtype),
        ),
        in_specs=[any_spec, any_spec],
        out_specs=(any_spec, any_spec),
        scratch_shapes=[
            pltpu.SemaphoreType.DMA((3,)),
            pltpu.SemaphoreType.DMA((3,)),
            pltpu.SemaphoreType.DMA((n - 1, PIECES)),
            pltpu.SemaphoreType.DMA((n - 1, PIECES)),
        ],
        input_output_aliases={0: 0, 1: 1},
        compiler_params=pltpu.CompilerParams(collective_id=which, has_side_effects=True),
        name="exchange",
    )(amps, ints)


def spread_kernel(n, b_ref, out_ref, own_sem, send_sem, recv_sem):
    o = lax.axis_index("occ")
    v = lax.axis_index("vir")
    mesh_id = pl.DeviceIdType.MESH
    rows = SQUARE // n

    def part(owner):
        return b_ref.at[pl.ds(pl.multiple_of(owner * rows, rows), rows)]

    barrier = pltpu.get_barrier_semaphore()
    for away in range(1, n):
        pl.semaphore_signal(
            barrier, inc=1, device_id=((o + away) % n, v), device_id_type=mesh_id
        )
    pl.semaphore_wait(barrier, n - 1)
    copies = []
    for away in range(1, n):
        target = (o + away) % n
        copies.append(
            pltpu.make_async_remote_copy(
                src_ref=part(target),
                dst_ref=out_ref.at[o],
                send_sem=send_sem.at[away - 1],
                recv_sem=recv_sem.at[away - 1],
                device_id=(target, v),
                device_id_type=mesh_id,
            )
        )
        copies[-1].start()
    own = pltpu.make_async_copy(part(o), out_ref.at[o], own_sem)
    own.start()
    for copy in copies:
        copy.wait_recv()
    for copy in copies:
        copy.wait_send()
    own.wait()


def spread(n, which, integrals):
    any_spec = pl.BlockSpec(memory_space=pl.ANY)
    return pl.pallas_call(
        functools.partial(spread_kernel, n),
        out_shape=jax.ShapeDtypeStruct((n, SQUARE // n, 2 * SQUARE), integrals.dtype),
        in_specs=[any_spec],
        out_specs=any_spec,
        scratch_shapes=[
            pltpu.SemaphoreType.DMA,
            pltpu.SemaphoreType.DMA((n - 1,)),
            pltpu.SemaphoreType.DMA((n - 1,)),
        ],
        compiler_params=pltpu.CompilerParams(collective_id=which, has_side_effects=True),
        name="spread",
    )(integrals)


def select_kernel(index_ref, part_ref, slot_ref):
    slot_ref[...] = part_ref[...]


def select(index, place, parts, slots):
    n, rows = parts.shape[:2]
    last = index.shape[0]
    return pl.pallas_call(
        select_kernel,
        out_shape=jax.ShapeDtypeStruct((2 * n, SQUARE, SQUARE), parts.dtype),
        grid_spec=pltpu.PrefetchScalarGridSpec(
            num_scalar_prefetch=1,
            grid=(slots,),
            in_specs=[pl.BlockSpec((1, rows, SQUARE), lambda j, ix: (ix[j] // 2, 0, ix[j] % 2))],
            out_specs=pl.BlockSpec((1, rows, SQUARE), lambda j, ix: (j, ix[last], 0)),
        ),
        name="select",
    )(jnp.concatenate([index, place[None]]), parts)


def by_slots(n, which, cap_a, cap_b, amplitudes, integrals, a_index, b_index, all_index):
    amps = pack(a_index, lax.axis_index("vir"), amplitudes, cap_a, (4, 4))
    ints = pack(b_index, lax.axis_index("occ"), integrals, cap_b, (n, 2))
    window = functools.partial(slot_window, cap_b)
    amps, ints = exchange(n, which, cap_a, window, amps, ints)
    return amps, ints.reshape(2 * n, SQUARE, SQUARE)


def by_slices(n, which, cap_a, slots, amplitudes, integrals, a_index, b_index, all_index):
    parts = spread(n, which, integrals)
    amps = pack(a_index, lax.axis_index("vir"), amplitudes, cap_a, (4, 4))
    ints = select(all_index, lax.axis_index("occ"), parts, slots)
    window = functools.partial(slice_window, n, slots)
    return exchange(n, which + 1, cap_a, window, amps, ints)


def ladder_kernel(
    steps,
    at_ref,
    count_ref,
    keep_ref,
    a_slot,
    b_slot,
    a_ref,
    b_ref,
    other_ref,
    occ_ref,
    vir_ref,
    out_ref,
    acc,
):
    at = at_ref[pl.program_id(0)]
    live = pl.program_id(0) < at_ref[4 * steps]
    block = at // steps
    step = at % steps
    count = count_ref[block]
    a_block = a_ref.at[0]
    b_block = b_ref.at[0]

    @pl.when(live & (step == 0))
    def _():
        acc[...] = jnp.zeros_like(acc)

    @pl.when(live & (step < count))
    def _():
        @pl.loop(0, SQUARE // STEP_COLS)
        def _(part):
            cols = pl.ds(pl.multiple_of(part * STEP_COLS, STEP_COLS), STEP_COLS)
            acc[:, cols] += jnp.dot(
                a_block[...], b_block[:, cols], preferred_element_type=jnp.float32
            )

    last = live & (step == jnp.maximum(count, 1) - 1)

    @pl.when(last & (keep_ref[block] == 1))
    def _():
        @pl.loop(0, SQUARE // 128)
        def _(part):
            cut = pl.ds(pl.multiple_of(part * 128, 128), 128)
            denom = occ_ref[0, cut, :] - vir_ref[0]
            total = acc[cut, :] + other_ref[cut, :].astype(jnp.float32)
            out_ref[cut, :] = (total / denom).astype(out_ref.dtype)

    @pl.when(last & (keep_ref[block] == 0))
    def _():
        out_ref[...] = jnp.zeros_like(out_ref)


def ladder(count, keep, a_slot, b_slot, steps, a_all, b_all, other_terms, occ_sum, vir_sum):
    ends = jnp.sum(
        jnp.where(jnp.arange(4)[:, None] <= jnp.arange(4)[None, :], jnp.maximum(count, 1)[:, None], 0),
        axis=0,
    )
    flat = jnp.minimum(jnp.arange(4 * steps, dtype=jnp.int32), ends[3] - 1)
    past = flat[:, None] >= ends[None, :3]
    start = jnp.max(jnp.where(past, ends[None, :3], 0), axis=1)
    block = jnp.sum(past.astype(jnp.int32), axis=1)
    at = jnp.concatenate([block * steps + flat - start, ends[3:]]).astype(jnp.int32)
    operands = (at, count, keep, a_slot, b_slot, a_all, b_all, other_terms, occ_sum, vir_sum)
    sizes = (6, 12, 4 * steps)
    return lax.switch(
        jnp.sum((ends[3] > jnp.array(sizes[:2])).astype(jnp.int32)),
        [functools.partial(ladder_call, steps, size) for size in sizes],
        *operands,
    )


def ladder_call(steps, size, *operands):
    square = (SQUARE, SQUARE)
    other_terms = operands[7]
    return pl.pallas_call(
        functools.partial(ladder_kernel, steps),
        out_shape=jax.ShapeDtypeStruct(other_terms.shape, other_terms.dtype),
        grid_spec=pltpu.PrefetchScalarGridSpec(
            num_scalar_prefetch=5,
            grid=(size,),
            in_specs=[
                pl.BlockSpec((1,) + square, lambda i, t, c, k, sa, sb: (sa[t[i]], 0, 0)),
                pl.BlockSpec((1,) + square, lambda i, t, c, k, sa, sb: (sb[t[i]], 0, 0)),
                pl.BlockSpec(
                    square, lambda i, t, c, k, sa, sb: (t[i] // steps // 2, t[i] // steps % 2)
                ),
                pl.BlockSpec(
                    (1, SQUARE, 1), lambda i, t, c, k, sa, sb: (t[i] // steps // 2, 0, 0)
                ),
                pl.BlockSpec(
                    (1, 1, SQUARE), lambda i, t, c, k, sa, sb: (t[i] // steps % 2, 0, 0)
                ),
            ],
            out_specs=pl.BlockSpec(
                square, lambda i, t, c, k, sa, sb: (t[i] // steps // 2, t[i] // steps % 2)
            ),
            scratch_shapes=[pltpu.VMEM(square, jnp.float32)],
        ),
        compiler_params=pltpu.CompilerParams(vmem_limit_bytes=60 << 20),
        name="ladder",
    )(*operands)


def ranks(flags):
    size = flags.shape[-1]
    before = jnp.arange(size)[:, None] < jnp.arange(size)[None, :]
    return jnp.sum(jnp.where(before, flags[..., :, None], 0), axis=-2)


def pick(flags, rank, values, size):
    total = jnp.sum(flags, axis=-1, keepdims=True)
    want = jnp.minimum(jnp.arange(size), jnp.maximum(total - 1, 0))
    hit = (flags[..., :, None] == 1) & (rank[..., :, None] == want[..., None, :])
    return jnp.sum(jnp.where(hit, values[..., :, None], 0), axis=-2)


def block_device(
    amplitudes,
    integrals,
    other_terms,
    occ_irrep,
    vir_irrep,
    pair_tiles,
    spin_mask,
    occ_energy,
    vir_energy,
):
    o = lax.axis_index("occ")
    v = lax.axis_index("vir")
    allowed, _ = symmetry(occ_irrep, vir_irrep, pair_tiles, spin_mask)
    allowed = allowed.astype(jnp.int32)
    pairs = allowed.shape[1]
    occ_devices = allowed.shape[0] // 2
    used = jnp.max(allowed[:, :, None] * allowed[:, None, :], axis=0)
    a_flags = allowed.reshape(occ_devices, 2, 4, 2).transpose(0, 2, 1, 3).reshape(occ_devices, 4, 4)
    b_flags = used.reshape(pairs, 4, 2)
    a_most = jnp.max(jnp.sum(a_flags, axis=-1))
    b_most = jnp.max(jnp.sum(b_flags, axis=-1))

    a_here = lax.dynamic_index_in_dim(a_flags, o, 0, keepdims=False)
    a_rank = ranks(a_here)
    b_here = lax.dynamic_index_in_dim(b_flags, v, 1, keepdims=False)
    b_rank = ranks(b_here)
    a_mine = lax.dynamic_index_in_dim(a_here, v, 0, keepdims=False)
    b_mine = lax.dynamic_index_in_dim(b_here, o, 0, keepdims=False)
    a_index = pick(a_mine, ranks(a_mine), jnp.arange(4, dtype=jnp.int32), 4)
    b_index = pick(b_mine, ranks(b_mine), jnp.arange(2, dtype=jnp.int32), 2)

    all_flags = b_here.reshape(-1)
    all_rank = ranks(all_flags)
    all_index = pick(all_flags, all_rank, jnp.arange(2 * pairs, dtype=jnp.int32), 8)
    all_most = jnp.max(jnp.sum(b_flags, axis=(0, 2)))

    wide = (a_most > 2).astype(jnp.int32)
    sliced = (b_most > 1) & (all_most <= 8)
    by_slice = jnp.where((all_most <= 6) & (a_most <= 2), 3, 4 + wide)
    variant = jnp.where(sliced, by_slice, jnp.where(b_most > 1, 2, wide))
    slots = functools.partial(by_slots, occ_devices)
    slices = functools.partial(by_slices, occ_devices)
    a_all, b_all = lax.switch(
        variant,
        [
            functools.partial(slots, 0, 2, 1),
            functools.partial(slots, 1, 4, 1),
            functools.partial(slots, 2, 4, 2),
            functools.partial(slices, 3, 2, 6),
            functools.partial(slices, 5, 2, 8),
            functools.partial(slices, 7, 4, 8),
        ],
        amplitudes,
        integrals,
        a_index,
        b_index,
        all_index,
    )

    a_rows = a_here.reshape(4, 2, 2).transpose(1, 0, 2).reshape(2, pairs)
    a_at = (a_rank + 4 * jnp.arange(4, dtype=jnp.int32)[:, None]).reshape(4, 2, 2)
    a_at = a_at.transpose(1, 0, 2).reshape(2, pairs)
    b_at = b_rank + 2 * jnp.arange(pairs, dtype=jnp.int32)[:, None]
    b_at = jnp.where(sliced, all_rank.reshape(pairs, 2), b_at).T
    keep = a_mine.reshape(2, 2)
    terms = a_rows[:, None, :] * keep[:, :, None]
    order = ranks(terms)
    a_slot = pick(terms, order, jnp.broadcast_to(a_at[:, None, :], terms.shape), pairs)
    b_slot = pick(terms, order, jnp.broadcast_to(b_at[None, :, :], terms.shape), pairs)
    count = jnp.sum(terms, axis=-1).reshape(-1)

    occ_tiles = occ_energy.reshape(OTILES, TILE)
    pair_occ = (occ_tiles[:, None, :, None] + occ_tiles[None, :, None, :]).reshape(-1, SQUARE)
    occ_sum = lax.dynamic_slice_in_dim(pair_occ, 2 * o, 2, 0)[:, :, None]
    vir_tiles = vir_energy.reshape(-1, TILE)
    tiles = lax.dynamic_slice_in_dim(pair_tiles, 2 * v, 2, 0)
    first = lookup(tiles[:, 0], vir_tiles)
    second = lookup(tiles[:, 1], vir_tiles)
    vir_sum = (first[:, :, None] + second[:, None, :]).reshape(2, 1, SQUARE)

    return ladder(
        count,
        keep.reshape(-1),
        a_slot.reshape(-1),
        b_slot.reshape(-1),
        pairs,
        a_all.reshape(-1, SQUARE, SQUARE),
        b_all,
        other_terms,
        occ_sum,
        vir_sum,
    )


def per_device(amplitudes, integrals, *rest):
    blocks = amplitudes.shape == (2 * SQUARE, 2 * SQUARE)
    blocks = blocks and integrals.shape == (SQUARE, 2 * SQUARE) and lax.axis_size("vir") == 4
    blocks = blocks and lax.axis_size("occ") == OTILES * OTILES // 2
    device = block_device if blocks else dense_device
    return device(amplitudes, integrals, *rest)


def solution(mesh):
    in_specs = (P("occ", "vir"), P("occ", "vir"), P("occ", "vir"), P(), P(), P(), P(), P(), P())
    out_specs = P("occ", "vir")
    return jax.shard_map(
        per_device, mesh=mesh, in_specs=in_specs, out_specs=out_specs, check_vma=False
    )
```
